32 devices in a mesh: dom: 2 (over y), blk: 4 (over z), sub: 2 (over x), rep: 2 (over core).
Axes of the slice: x: 2, y: 2, z: 4, core: 2. Of those that a mesh axis runs over, the one named last changes fastest.
Arguments:
- tokens: bfloat16 [4096, 2048], P(('dom', 'blk', 'sub', 'rep')), parts along dimension 0, may hold values from -6 to 6
- expert_ids: int32 [4096, 8], P(('dom', 'blk', 'sub', 'rep')), parts along dimension 0, may hold values from 0 to 127, as said below
- gate_weights: float32 [4096, 8], P(('dom', 'blk', 'sub', 'rep')), parts along dimension 0, may hold values from 0.2 to 2
- w_gate: bfloat16 [2, 768, 2048], P('sub', 'rep', 'blk'), may hold values from -0.125 to 0.125
- w_up: bfloat16 [2, 768, 2048], P('sub', 'rep', 'blk'), may hold values from -0.125 to 0.125
- w_down: bfloat16 [2, 768, 2048], P('sub', 'rep', 'blk'), may hold values from -0.21875 to 0.21875
- cotangent: bfloat16 [4096, 2048], P(('dom', 'blk', 'sub', 'rep')), parts along dimension 0, may hold values from -6 to 6
Outputs:
- mixed: bfloat16 [4096, 2048], P(('dom', 'blk', 'sub', 'rep')), parts along dimension 0
- token_grad: bfloat16 [4096, 2048], P(('dom', 'blk', 'sub', 'rep')), parts along dimension 0
- gate_grad: float32 [4096, 8], P(('dom', 'blk', 'sub', 'rep')), parts along dimension 0
- grad_gate: float32 [4, 768, 2048], P(('dom', 'sub'), 'rep', 'blk'), parts along dimension 0
- grad_up: float32 [4, 768, 2048], P(('dom', 'sub'), 'rep', 'blk'), parts along dimension 0
- grad_down: float32 [4, 768, 2048], P(('dom', 'sub'), 'rep', 'blk'), parts along dimension 0
The draws below stay inside these ranges and needn't reach their ends.
There are 2 independent parts, one for each index of `dom`. The reference program is written for one: setup_inputs(seed, part) draws one part's arguments, and reference() takes and returns one part's arrays. A program takes and returns all parts, laid end to end along the dimension named above; an argument that names none is the same for every part. Nothing has to cross between parts.
Inputs may be any that keep to these rules, and one draw needn't show every extreme that they name: `expert_ids`: each row names 8 different experts. Among the 128 rows of one device, each expert below 2 is named by 1 to 12 rows, and in every draw some expert below 2 is named by 12 rows on every device of one blk index.
All inputs are finite; a program needn't handle non-finite values.
Results may differ from the reference program's by a relative error of at most 0.02.
Values may be sent and summed in bfloat16 or wider, within the bound.
No kernel may reach another device: no remote copies, remote signals or barrier semaphores. Data moves between devices by JAX's collectives and lax.ppermute only.
A program may use at most 64 MiB of HBM per device.

```python
import math
import jax
import jax.numpy as jnp
from jax import lax

D = 2048
FF = 768
NUM_EXPERTS = 128
TOPK = 8
TOK_DEV = 128
CAP = 12
EXP_WIN = 2
LOOP_LEN = 4
SUB_LEN = 2
REP_LEN = 2
TOKENS = 2048


def draw_expert_ids(key, part):
    blocks = TOKENS // TOK_DEV
    key_count = jax.random.fold_in(key, 21)
    key_hot_blk = jax.random.fold_in(key, 22)
    key_hot_exp = jax.random.fold_in(key, 24)
    key_pick = jax.random.fold_in(key, 25)
    key_fill = jax.random.fold_in(key, 26)
    key_place = jax.random.fold_in(key, 27)
    counts = jax.random.randint(key_count, (LOOP_LEN, SUB_LEN, REP_LEN, EXP_WIN), 1, CAP + 1).astype(jnp.int32)
    hot_blk = jax.random.randint(key_hot_blk, (), 0, LOOP_LEN)
    hot_exp = jax.random.randint(key_hot_exp, (), 0, EXP_WIN)
    blk_iota = jnp.arange(LOOP_LEN, dtype=jnp.int32)[:, None, None, None]
    exp_iota = jnp.arange(EXP_WIN, dtype=jnp.int32)[None, None, None, :]
    full_group = (blk_iota == hot_blk) & (exp_iota == hot_exp)
    counts = jnp.where(full_group, CAP, counts).reshape(blocks, EXP_WIN)
    scores = jax.random.randint(key_pick, (blocks, EXP_WIN, TOK_DEV), 0, 1 << 20) * TOK_DEV + jnp.arange(TOK_DEV, dtype=jnp.int32)
    token_ranks = jnp.argsort(jnp.argsort(scores, axis=2), axis=2)
    chosen = token_ranks < counts[:, :, None]
    chosen = jnp.transpose(chosen, (0, 2, 1)).reshape(TOKENS, EXP_WIN)
    spare = NUM_EXPERTS - EXP_WIN
    fill_scores = jax.random.randint(key_fill, (TOKENS, spare), 0, 1 << 20) * NUM_EXPERTS + jnp.arange(spare, dtype=jnp.int32)
    chosen_ids = jnp.argsort(fill_scores, axis=1)[:, :TOPK].astype(jnp.int32) + EXP_WIN
    place_scores = jax.random.randint(key_place, (TOKENS, TOPK), 0, 1 << 20) * TOPK + jnp.arange(TOPK, dtype=jnp.int32)
    places = jnp.argsort(place_scores, axis=1).astype(jnp.int32)
    topk_iota = jnp.arange(TOPK, dtype=jnp.int32)[None, :]
    for expert in range(EXP_WIN):
        landing = (topk_iota == places[:, expert:expert + 1]) & chosen[:, expert:expert + 1]
        chosen_ids = jnp.where(landing, expert, chosen_ids)
    return chosen_ids.astype(jnp.int32)


def shard_levels(own_key, dims, split, smallest, high):
    level, own = 1.0, jax.random.fold_in(own_key, 6)
    for position, shards_of in split:
        draws = jnp.exp(jax.random.uniform(jax.random.fold_in(own, position), (shards_of,), jnp.float32, smallest / len(split), high / len(split)))
        level = level * jnp.repeat(draws, dims[position] // shards_of).reshape([-1 if axis == position else 1 for axis in range(len(dims))])
    return level


def scatter_about(key, shape, scale, reach, cuts=(), kind=jnp.bfloat16):
    values = jax.random.normal(key, shape, jnp.float32) * scale
    if len(cuts) > 0:
        values = shard_levels(key, shape, cuts, -0.22, 0.18) * values
    return jnp.clip(values, min=-reach, max=reach).astype(kind)


def setup_inputs(seed: int = 0, part: int = 0) -> dict:
    seeds = jax.random.split(jax.random.key(seed), 8)
    part_keys = jax.random.split(jax.random.fold_in(seeds[7], part), 8)
    tokens = scatter_about(part_keys[0], (TOKENS, D), 1.0, 6.0, ((0, 16),))
    expert_ids = draw_expert_ids(jax.random.fold_in(jax.random.fold_in(seeds[7], part), 71), part)
    gate_weights = jnp.clip(jnp.exp(math.log(2.0) - 2.3025851 * jax.random.uniform(part_keys[2], (TOKENS, TOPK), jnp.float32) ** shard_levels(part_keys[2], (TOKENS, TOPK), ((0, 16),), -0.2, 0.2)), 0.2, 2.0)
    w_gate = scatter_about(seeds[3], (EXP_WIN, FF, D), D ** -0.5, 0.125, ((0, 2), (1, 2), (2, 4)))
    w_up = scatter_about(seeds[4], (EXP_WIN, FF, D), D ** -0.5, 0.125, ((0, 2), (1, 2), (2, 4)))
    w_down = scatter_about(seeds[5], (EXP_WIN, FF, D), FF ** -0.5, 0.21875, ((0, 2), (1, 2), (2, 4)))
    cotangent = scatter_about(part_keys[6], (TOKENS, D), 1.0, 6.0, ((0, 16),))
    return {"tokens": tokens, "expert_ids": expert_ids, "gate_weights": gate_weights, "w_gate": w_gate, "w_up": w_up, "w_down": w_down, "cotangent": cotangent}


def silu_pair(pre_act):
    sigmoid_v = jax.nn.sigmoid(pre_act)
    return (pre_act * sigmoid_v, sigmoid_v * (1.0 + pre_act * (1.0 - sigmoid_v)))

def slot_table(expert_ids, expert):
    blocks = TOKENS // TOK_DEV
    named_hits = expert_ids == expert
    picked = lax.optimization_barrier(jnp.sum(named_hits.astype(jnp.int32), axis=1)).astype(jnp.int32).reshape(blocks, TOK_DEV)
    before = (jnp.cumsum(picked, axis=1).astype(jnp.int32) - picked).astype(jnp.int32)
    slot_iota = jnp.arange(CAP, dtype=jnp.int32)
    placed = (before[:, None, :] == slot_iota[None, :, None]) & (picked[:, None, :] > 0)
    local_iota = jnp.arange(TOK_DEV, dtype=jnp.int32)
    local_row = lax.optimization_barrier(jnp.sum(jnp.where(placed, local_iota[None, None, :], 0), axis=2)).astype(jnp.int32)
    offsets = (jnp.arange(blocks, dtype=jnp.int32) * TOK_DEV)[:, None]
    row_index = (local_row + offsets).reshape(-1).astype(jnp.int32)
    valid_row = jnp.any(placed, axis=2).reshape(-1)
    return (named_hits, row_index, valid_row)

def half_sum(left_a, right_a, left_b, right_b):
    slice_len = FF // REP_LEN
    result = jnp.zeros((left_a.shape[0], D), jnp.float32)
    for block in range(REP_LEN):
        lower = block * slice_len
        partial_value = jnp.dot(left_a[:, lower:lower + slice_len], right_a[lower:lower + slice_len], preferred_element_type=jnp.float32)
        if left_b is not None:
            partial_value = partial_value + jnp.dot(left_b[:, lower:lower + slice_len], right_b[lower:lower + slice_len], preferred_element_type=jnp.float32)
        result = result + lax.optimization_barrier(partial_value.astype(jnp.bfloat16)).astype(jnp.float32)
    return lax.optimization_barrier(result.astype(jnp.bfloat16)).astype(jnp.float32)

def group_grad(left, right, grad_scale):
    left_rows = left.astype(jnp.float32).reshape(LOOP_LEN, -1, left.shape[1])
    right_rows = right.astype(jnp.float32).reshape(LOOP_LEN, -1, right.shape[1])
    parts = jnp.einsum('brf,brd->bfd', left_rows, right_rows, precision=lax.Precision.HIGHEST) * grad_scale
    return lax.optimization_barrier(jnp.sum(lax.optimization_barrier(parts.astype(jnp.bfloat16)).astype(jnp.float32), axis=0))

def reference(tokens, expert_ids, gate_weights, w_gate, w_up, w_down, cotangent):
    grad_scale = (TOKENS * TOPK / NUM_EXPERTS) ** (-0.5)
    mixed_sum = jnp.zeros((TOKENS, D), jnp.float32)
    input_sum = jnp.zeros((TOKENS, D), jnp.float32)
    gate_grad = jnp.zeros((TOKENS, TOPK), jnp.float32)
    grads_gate = []
    grads_up = []
    grads_down = []
    for expert in range(EXP_WIN):
        named_hits, row_index, valid_row = slot_table(expert_ids, expert)
        weight_of = lax.optimization_barrier(jnp.sum(jnp.where(named_hits, gate_weights, jnp.zeros((), jnp.float32)), axis=1))
        row_weight = jnp.where(valid_row, weight_of[row_index], jnp.zeros((), jnp.float32))
        row_tokens = jnp.where(valid_row[:, None], tokens[row_index], jnp.zeros((), jnp.bfloat16))
        row_cotan = jnp.where(valid_row[:, None], cotangent[row_index], jnp.zeros((), jnp.bfloat16))
        pre_gate = jnp.dot(row_tokens, w_gate[expert].T, preferred_element_type=jnp.float32)
        pre_up = jnp.dot(row_tokens, w_up[expert].T, preferred_element_type=jnp.float32)
        activated, silu_slope = silu_pair(pre_gate)
        hidden = (activated * pre_up).astype(jnp.bfloat16)
        expert_out = half_sum(hidden, w_down[expert], None, None)
        mixed_sum = mixed_sum.at[row_index].add(row_weight[:, None] * expert_out)
        row_dot = lax.optimization_barrier(jnp.sum(row_cotan.astype(jnp.float32) * expert_out, axis=1))
        token_dot = jnp.zeros((TOKENS,), jnp.float32).at[row_index].add(jnp.where(valid_row, row_dot, jnp.zeros((), jnp.float32)))
        gate_grad = gate_grad + jnp.where(named_hits, token_dot[:, None], jnp.zeros((), jnp.float32))
        row_dout = (row_weight[:, None] * row_cotan.astype(jnp.float32)).astype(jnp.bfloat16)
        dhidden = jnp.dot(row_dout, w_down[expert].T, preferred_element_type=jnp.float32)
        dpre_gate = (dhidden * pre_up * silu_slope).astype(jnp.bfloat16)
        dpre_up = (dhidden * activated).astype(jnp.bfloat16)
        input_rows = half_sum(dpre_gate, w_gate[expert], dpre_up, w_up[expert])
        input_sum = input_sum.at[row_index].add(input_rows)
        grads_gate.append(group_grad(dpre_gate, row_tokens, grad_scale))
        grads_up.append(group_grad(dpre_up, row_tokens, grad_scale))
        grads_down.append(group_grad(hidden, row_dout, grad_scale))
    return (mixed_sum.astype(jnp.bfloat16), input_sum.astype(jnp.bfloat16), gate_grad, jnp.stack(grads_gate), jnp.stack(grads_up), jnp.stack(grads_down))
```

```python
import functools

import jax
import jax.numpy as jnp
from jax import lax
from jax.experimental import pallas as pl
from jax.experimental.pallas import tpu as pltpu
from jax.sharding import PartitionSpec as P

NUM_EXPERTS = 128
CAP = 12
MAX_DIRECT = 8


F32 = jnp.float32
BF16 = jnp.bfloat16


def iota(shape, dim):
    return lax.broadcasted_iota(jnp.int32, shape, dim)


def group_of(index, size, groups):
    result = jnp.zeros_like(index)
    for start in range(1, groups):
        result = result + (index >= start * size).astype(jnp.int32)
    return result


def dot(a, b, ca=1, cb=0):
    return lax.dot_general(a, b, (((ca,), (cb,)), ((), ())), preferred_element_type=F32)


def slot_rows(ids_ref, gate_ref, own_sub, n_sub):
    top_k, tok = ids_ref.shape
    n_rows = n_sub * 2 * CAP
    row = iota((n_rows, tok), 0)
    part = group_of(row, 2 * CAP, n_sub)
    rest = row - part * (2 * CAP)
    second = rest >= CAP
    slot = rest - jnp.where(second, CAP, 0)
    expert = lax.bitwise_xor(part, own_sub)
    picked = jnp.zeros((n_rows, tok), F32)
    weight = jnp.zeros((n_rows, tok), F32)
    for k in range(top_k):
        hit = ids_ref[k : k + 1, :] == expert
        picked = picked + jnp.where(hit, 1.0, 0.0)
        weight = weight + jnp.where(hit, gate_ref[k : k + 1, :], 0.0)
    earlier = (iota((tok, tok), 0) < iota((tok, tok), 1)).astype(F32).astype(BF16)
    before = dot(picked.astype(BF16), earlier)
    placed = (before == slot.astype(F32)) & (picked > 0.5)
    return jnp.where(placed, 1.0, 0.0), weight, part, second


def pair_matrix(n_sub, back):
    n = n_sub * 2 * CAP
    out_row, in_row = iota((n, n), 0), iota((n, n), 1)
    mixed_row, plain_row = (in_row, out_row) if back else (out_row, in_row)
    kind = (mixed_row >= n_sub * CAP).astype(jnp.int32)
    rest = mixed_row - kind * (n_sub * CAP)
    where_to = rest + CAP * group_of(rest, CAP, n_sub) + CAP * kind
    return (where_to == plain_row).astype(F32).astype(BF16)


def route_kernel(n_blk, n_sub, direct, place_ref, ids_ref, gate_ref, tokens_ref, cotan_ref, *rest):
    send, rows_ref = rest[:-1], rest[-1]
    send = send if direct else [send[0].at[i] for i in range(n_blk * n_sub)]
    width = tokens_ref.shape[1] // n_blk
    own_blk, own_sub = place_ref[0], place_ref[1]
    placed, weight, _, second = slot_rows(ids_ref, gate_ref, own_sub, n_sub)
    gate = jnp.sum(placed * weight, axis=1, keepdims=True)
    low = placed.astype(BF16)
    is_cotan = second[:, :1]
    rows = dot(low, tokens_ref[...])
    dout = dot(low, cotan_ref[...]) * gate
    rows_ref[...] = jnp.where(is_cotan, dout, rows)
    for mb in range(n_blk):
        start = pl.multiple_of(lax.bitwise_xor(mb, own_blk) * width, 128)
        for ms in range(n_sub):
            block = rows_ref[ms * 2 * CAP : (ms + 1) * 2 * CAP, pl.ds(start, width)]
            send[mb * n_sub + ms][...] = block.astype(BF16)


def first_kernel(n_blk, n_sub, direct, *refs):
    n = n_blk * n_sub
    n_in = n if direct else 1
    recv = refs[:n] if direct else [refs[0].at[i] for i in range(n)]
    wg_ref, wu_ref, wd_ref, xg_ref, xu_ref, xd_ref = refs[n_in : n_in + 6]
    both_ref = refs[n_in + 6]
    sends = refs[n_in + 7 : -1]
    sends = sends if direct else [sends[0].at[i] for i in range(n_blk)]
    rows_ref = refs[-1]
    rows = n_sub * CAP
    total = n_blk * rows
    order = pair_matrix(n_sub, False)
    for mb in range(n_blk):
        block = jnp.concatenate([recv[mb * n_sub + ms][...].astype(F32) for ms in range(n_sub)], axis=0)
        moved = dot(order, block.astype(BF16))
        rows_ref[mb * rows : (mb + 1) * rows, :] = moved[:rows]
        rows_ref[total + mb * rows : total + (mb + 1) * rows, :] = moved[rows:]
    both_ref[...] = rows_ref[...].astype(BF16)
    toks, dout = both_ref[:total, :], both_ref[total:, :]
    ff = wg_ref.shape[0]
    for i, (left, right) in enumerate(
        ((toks, wg_ref), (toks, xg_ref), (toks, wu_ref), (toks, xu_ref), (dout, wd_ref), (dout, xd_ref))
    ):
        part = dot(left, right[...], 1, 1)
        for mb in range(n_blk):
            sends[mb][:, i * ff : (i + 1) * ff] = part[mb * rows : (mb + 1) * rows].astype(BF16)


def act_kernel(n_blk, direct, *refs):
    recv = refs[:-1] if direct else [refs[0].at[i] for i in range(n_blk)]
    out_ref = refs[-1]
    ff = out_ref.shape[1] // 3
    total = recv[0][...].astype(F32)
    for i in range(1, n_blk):
        total = total + recv[i][...].astype(F32)
    gate, up, dhid = total[:, :ff], total[:, ff : 2 * ff], total[:, 2 * ff :]
    sig = jax.nn.sigmoid(gate)
    silu = gate * sig
    slope = sig * (1.0 + gate * (1.0 - sig))
    out_ref[:, :ff] = (silu * up).astype(BF16)
    out_ref[:, ff : 2 * ff] = (dhid * up * slope).astype(BF16)
    out_ref[:, 2 * ff :] = (dhid * silu).astype(BF16)


def second_kernel(n_blk, n_sub, direct, *refs):
    n_in = n_blk if direct else 1
    recv = refs[:n_blk] if direct else [refs[0].at[i] for i in range(n_blk)]
    wg_ref, wu_ref, wd_ref, xg_ref, xu_ref, xd_ref = refs[n_in : n_in + 6]
    own_ref, other_ref = refs[n_in + 6 : n_in + 8]
    sends = refs[n_in + 8 : -1]
    sends = sends if direct else [sends[0].at[i] for i in range(n_blk * n_sub)]
    rows_ref = refs[-1]
    rows = n_sub * CAP
    ff = wg_ref.shape[0]
    for mb in range(n_blk):
        rows_ref[mb * rows : (mb + 1) * rows, :] = recv[mb][...].astype(F32)
    for i in range(3):
        own_ref[:, i * ff : (i + 1) * ff] = rows_ref[:, 2 * i * ff : (2 * i + 1) * ff].astype(BF16)
        other_ref[:, i * ff : (i + 1) * ff] = rows_ref[:, (2 * i + 1) * ff : (2 * i + 2) * ff].astype(BF16)
    out = dot(own_ref[:, :ff], wd_ref[...]) + dot(other_ref[:, :ff], xd_ref[...])
    inp = (
        dot(own_ref[:, ff : 2 * ff], wg_ref[...])
        + dot(other_ref[:, ff : 2 * ff], xg_ref[...])
        + dot(own_ref[:, 2 * ff :], wu_ref[...])
        + dot(other_ref[:, 2 * ff :], xu_ref[...])
    )
    order = pair_matrix(n_sub, True)
    for mb in range(n_blk):
        lower, upper = mb * rows, (mb + 1) * rows
        block = jnp.concatenate([out[lower:upper], inp[lower:upper]], axis=0).astype(BF16)
        moved = dot(order, block)
        for ms in range(n_sub):
            sends[mb * n_sub + ms][...] = moved[ms * 2 * CAP : (ms + 1) * 2 * CAP].astype(BF16)


def grad_kernel(scale, own_ref, peer_ref, both_ref, peer_both_ref, gg_ref, gu_ref, gd_ref):
    total = own_ref.shape[0]
    ff = own_ref.shape[1] // 3
    for i, (out_ref, lower) in enumerate(((gd_ref, total), (gg_ref, 0), (gu_ref, 0))):
        left = own_ref[:, i * ff : (i + 1) * ff]
        left_peer = peer_ref[:, i * ff : (i + 1) * ff]
        right = both_ref[lower : lower + total, :]
        right_peer = peer_both_ref[lower : lower + total, :]
        out_ref[0] = (dot(left, right, 0, 0) + dot(left_peer, right_peer, 0, 0)) * scale


def mix_kernel(n_blk, n_sub, direct, place_ref, ids_ref, gate_ref, cotan_ref, *refs):
    n = n_blk * n_sub
    recv = refs[:n] if direct else [refs[0].at[i] for i in range(n)]
    mixed_ref, grad_ref, gate_grad_ref = refs[-3:]
    tok, depth = cotan_ref.shape
    width = depth // n_blk
    own_blk, own_sub = place_ref[0], place_ref[1]
    placed, weight, part, second = slot_rows(ids_ref, gate_ref, own_sub, n_sub)
    first_rows = jnp.where(second, 0.0, placed)
    last_rows = jnp.where(second, placed, 0.0)
    pick_in = last_rows.T.astype(BF16)
    pick_out, weights, dots = [], [], []
    for ms in range(n_sub):
        mine = jnp.where(part == ms, first_rows, 0.0)
        pick_out.append(mine.T.astype(BF16))
        weights.append(jnp.sum((mine * weight).T, axis=1, keepdims=True))
        dots.append(jnp.zeros((tok, 1), F32))
    for mb in range(n_blk):
        start = pl.multiple_of(lax.bitwise_xor(mb, own_blk) * width, 128)
        block = jnp.concatenate(
            [recv[mb * n_sub + ms][...].astype(F32) for ms in range(n_sub)], axis=0
        ).astype(BF16)
        grad_ref[:, pl.ds(start, width)] = dot(pick_in, block).astype(BF16)
        cotan = cotan_ref[:, pl.ds(start, width)].astype(F32)
        mixed = jnp.zeros((tok, width), F32)
        for ms in range(n_sub):
            rows = dot(pick_out[ms], block)
            mixed = mixed + weights[ms] * rows
            dots[ms] = dots[ms] + jnp.sum(rows * cotan, axis=1, keepdims=True)
        mixed_ref[:, pl.ds(start, width)] = mixed.astype(BF16)
    same = iota((tok, tok), 0) == iota((tok, tok), 1)
    gate_grad = jnp.zeros(ids_ref.shape, F32)
    for ms in range(n_sub):
        line = jnp.sum(jnp.where(same, dots[ms], 0.0), axis=0, keepdims=True)
        hit = ids_ref[...] == lax.bitwise_xor(ms, own_sub)
        gate_grad = gate_grad + jnp.where(hit, line, 0.0)
    gate_grad_ref[...] = gate_grad


def call(kernel, out, args, scratch=(), flops=0, smem=0):
    def size(x):
        item = jnp.dtype(x.dtype).itemsize
        total = item
        for d in x.shape:
            total *= d
        return total

    moved = sum(size(x) for x in args) + sum(size(x) for x in out)
    limit = min(60 << 20, max(16 << 20, 3 * moved + sum(size(x) for x in scratch)))
    vmem = pl.BlockSpec(memory_space=pltpu.VMEM)
    return pl.pallas_call(
        kernel,
        out_shape=out,
        in_specs=[pl.BlockSpec(memory_space=pltpu.SMEM)] * smem + [vmem] * (len(args) - smem),
        out_specs=[vmem] * len(out),
        scratch_shapes=[pltpu.VMEM(x.shape, x.dtype) for x in scratch],
        compiler_params=pltpu.CompilerParams(vmem_limit_bytes=limit),
        cost_estimate=pl.CostEstimate(flops=flops, bytes_accessed=moved, transcendentals=0),
    )(*args)


def array(shape, dtype=BF16):
    return jax.ShapeDtypeStruct(shape, dtype)


def swap(x, axes, count, mask):
    return lax.ppermute(x, axes, [(i, i ^ mask) for i in range(count)])


def on_device(tokens, expert_ids, gate_weights, w_gate, w_up, w_down, cotangent):
    tok, depth = tokens.shape
    top_k = expert_ids.shape[1]
    n_blk, n_sub, n_rep = (lax.axis_size(a) for a in ("blk", "sub", "rep"))
    assert w_gate.shape[0] == 1 and n_rep == 2
    assert n_blk & (n_blk - 1) == 0 and n_sub & (n_sub - 1) == 0
    ff, width = w_gate.shape[1:]
    n = n_blk * n_sub
    direct = n <= MAX_DIRECT
    scale = (tok * n * n_rep * top_k / NUM_EXPERTS) ** (-0.5)
    rows = n_sub * CAP
    total = n_blk * rows
    pair = ("blk", "sub")
    place = jnp.stack([lax.axis_index("blk"), lax.axis_index("sub")]).astype(jnp.int32)
    if not direct:
        place = jnp.zeros_like(place)
    ids, gates = expert_ids.T, gate_weights.T
    weights = [w[0] for w in (w_gate, w_up, w_down)]
    weights = weights + [swap(w, "rep", 2, 1) for w in weights]

    def exchange(blocks, axes, count):
        if direct:
            return [b if m == 0 else swap(b, axes, count, m) for m, b in enumerate(blocks)]
        return [lax.all_to_all(blocks[0], axes, split_axis=0, concat_axis=0, tiled=True)]

    def blocks(count, shape):
        return [array(shape)] * count if direct else [array((count,) + shape)]

    sent = call(
        functools.partial(route_kernel, n_blk, n_sub, direct),
        blocks(n, (2 * CAP, width)),
        [place, ids, gates, tokens, cotangent],
        scratch=[array((n_sub * 2 * CAP, depth), F32)],
        smem=1,
    )
    got = exchange(sent, pair, n)
    both, *parts = call(
        functools.partial(first_kernel, n_blk, n_sub, direct),
        [array((2 * total, width))] + blocks(n_blk, (rows, 6 * ff)),
        list(got) + weights,
        scratch=[array((2 * total, width), F32)],
        flops=2 * total * width * 6 * ff,
    )
    both_peer = swap(both, "rep", 2, 1)
    parts = exchange(parts, "blk", n_blk)
    (act,) = call(
        functools.partial(act_kernel, n_blk, direct), [array((rows, 6 * ff))], list(parts)
    )
    if direct:
        acts = [act] + [swap(act, "blk", n_blk, m) for m in range(1, n_blk)]
    else:
        acts = [lax.all_gather(act, "blk", axis=0, tiled=False)]
    own, other, *sent = call(
        functools.partial(second_kernel, n_blk, n_sub, direct),
        [array((total, 3 * ff))] * 2 + blocks(n, (2 * CAP, width)),
        list(acts) + weights,
        scratch=[array((total, 6 * ff), F32)],
        flops=2 * total * width * 6 * ff,
    )
    got = exchange(sent, pair, n)
    peer = swap(other, "rep", 2, 1)
    grads = call(
        functools.partial(grad_kernel, scale),
        [array((1, ff, width), F32)] * 3,
        [own, peer, both, both_peer],
        flops=4 * total * width * 3 * ff,
    )
    mixed, token_grad, gate_grad = call(
        functools.partial(mix_kernel, n_blk, n_sub, direct),
        [array((tok, depth)), array((tok, depth)), array((top_k, tok), F32)],
        [place, ids, gates, cotangent] + list(got),
        smem=1,
    )
    return (mixed, token_grad, gate_grad.T, *grads)


def solution(mesh):
    by_token = P(("dom", "blk", "sub", "rep"), None)
    by_weight = P("sub", "rep", "blk")
    by_grad = P(("dom", "sub"), "rep", "blk")
    return jax.shard_map(
        on_device,
        mesh=mesh,
        in_specs=(by_token, by_token, by_token, by_weight, by_weight, by_weight, by_token),
        out_specs=(by_token, by_token, by_token, by_grad, by_grad, by_grad),
        check_vma=False,
    )
```

```python
import functools

import jax
import jax.numpy as jnp
from jax import lax
from jax.experimental import pallas as pl
from jax.experimental.pallas import tpu as pltpu
from jax.sharding import PartitionSpec as P

NUM_EXPERTS = 128
CAP = 12
MAX_DIRECT = 8
ORDER = [2, 3, 1]


F32 = jnp.float32
BF16 = jnp.bfloat16


def iota(shape, dim):
    return lax.broadcasted_iota(jnp.int32, shape, dim)


def group_of(index, size, groups):
    result = jnp.zeros_like(index)
    for start in range(1, groups):
        result = result + (index >= start * size).astype(jnp.int32)
    return result


def dot(a, b, ca=1, cb=0):
    return lax.dot_general(a, b, (((ca,), (cb,)), ((), ())), preferred_element_type=F32)


def slot_rows(ids_ref, gate_ref, n_sub):
    top_k, tok = ids_ref.shape
    n_rows = n_sub * 2 * CAP
    row = iota((n_rows, tok), 0)
    part = group_of(row, 2 * CAP, n_sub)
    rest = row - part * (2 * CAP)
    second = rest >= CAP
    slot = rest - jnp.where(second, CAP, 0)
    picked = jnp.zeros((n_rows, tok), F32)
    weight = jnp.zeros((n_rows, tok), F32)
    for k in range(top_k):
        hit = ids_ref[k : k + 1, :] == part
        picked = picked + jnp.where(hit, 1.0, 0.0)
        weight = weight + jnp.where(hit, gate_ref[k : k + 1, :], 0.0)
    earlier = (iota((tok, tok), 0) < iota((tok, tok), 1)).astype(F32).astype(BF16)
    before = dot(picked.astype(BF16), earlier)
    placed = (before == slot.astype(F32)) & (picked > 0.5)
    return jnp.where(placed, 1.0, 0.0), weight, part, second


def pair_matrix(n_sub, back):
    n = n_sub * 2 * CAP
    out_row, in_row = iota((n, n), 0), iota((n, n), 1)
    mixed_row, plain_row = (in_row, out_row) if back else (out_row, in_row)
    kind = (mixed_row >= n_sub * CAP).astype(jnp.int32)
    rest = mixed_row - kind * (n_sub * CAP)
    where_to = rest + CAP * group_of(rest, CAP, n_sub) + CAP * kind
    return (where_to == plain_row).astype(F32).astype(BF16)


def route_kernel(n_blk, n_sub, ids_hbm, gate_hbm, tokens_hbm, cotan_hbm, send_ref, ids_ref, gate_ref, tokens_ref, cotan_ref, sems):
    width = tokens_hbm.shape[1] // n_blk
    small = [
        pltpu.make_async_copy(ids_hbm, ids_ref, sems.at[0]),
        pltpu.make_async_copy(gate_hbm, gate_ref, sems.at[1]),
    ]
    large = []
    for mb in range(n_blk):
        columns = pl.ds(mb * width, width)
        for i, (source, target) in enumerate(((tokens_hbm, tokens_ref), (cotan_hbm, cotan_ref))):
            large.append(
                pltpu.make_async_copy(source.at[:, columns], target.at[:, columns], sems.at[2 + 2 * mb + i])
            )
    for copy in small + large:
        copy.start()
    for copy in small:
        copy.wait()
    placed, weight, _, second = slot_rows(ids_ref, gate_ref, n_sub)
    gate = jnp.sum(placed * weight, axis=1, keepdims=True)
    low = placed.astype(BF16)
    is_cotan = second[:, :1]
    for mb in range(n_blk):
        columns = pl.ds(mb * width, width)
        large[2 * mb].wait()
        rows = dot(low, tokens_ref[:, columns])
        large[2 * mb + 1].wait()
        dout = dot(low, cotan_ref[:, columns]) * gate
        block = jnp.where(is_cotan, dout, rows)
        for ms in range(n_sub):
            send_ref[mb * n_sub + ms] = block[ms * 2 * CAP : (ms + 1) * 2 * CAP].astype(BF16)


def views(refs, count):
    return list(refs) if len(refs) > 1 or count == 1 else [refs[0].at[i] for i in range(count)]


def block_start(mb, rows, n_blk):
    if n_blk > MAX_DIRECT:
        return mb * rows
    return pl.multiple_of(lax.bitwise_xor(lax.axis_index("blk").astype(jnp.int32), mb) * rows, 8)


def partial_products(n_blk, both_ref, weight_refs, part_ref, sends):
    total = both_ref.shape[0] // 2
    rows = total // n_blk
    ff = weight_refs[0].shape[0]
    toks, dout = both_ref[:total, :], both_ref[total:, :]
    for i, left in enumerate((toks, toks, dout)):
        part_ref[:, i * ff : (i + 1) * ff] = dot(left, weight_refs[i][...], 1, 1)
    for mb in range(n_blk):
        start = block_start(mb, rows, n_blk)
        sends[mb][...] = part_ref[pl.ds(start, rows), :].astype(BF16)


def first_kernel(n_blk, n_sub, recv_ref, *refs):
    weight_refs, both_ref = refs[:3], refs[3]
    sends, (part_ref, rows_ref) = views(refs[4:-2], n_blk), refs[-2:]
    rows = n_sub * CAP
    total = n_blk * rows
    order = pair_matrix(n_sub, False)
    for mb in range(n_blk):
        block = jnp.concatenate([recv_ref[mb * n_sub + ms].astype(F32) for ms in range(n_sub)], axis=0)
        moved = dot(order, block.astype(BF16))
        rows_ref[mb * rows : (mb + 1) * rows, :] = moved[:rows]
        rows_ref[total + mb * rows : total + (mb + 1) * rows, :] = moved[rows:]
    both_ref[...] = rows_ref[...].astype(BF16)
    partial_products(n_blk, both_ref, weight_refs, part_ref, sends)


def peer_kernel(n_blk, both_ref, *refs):
    partial_products(n_blk, both_ref, refs[:3], refs[-1], views(refs[3:-1], n_blk))


def act_kernel(n_blk, *refs):
    recv, out_ref = views(refs[:-1], n_blk), refs[-1]
    ff = out_ref.shape[1] // 3
    total = recv[0][...].astype(F32)
    for i in range(1, n_blk):
        total = total + recv[i][...].astype(F32)
    gate, up, dhid = total[:, :ff], total[:, ff : 2 * ff], total[:, 2 * ff :]
    sig = jax.nn.sigmoid(gate)
    silu = gate * sig
    slope = sig * (1.0 + gate * (1.0 - sig))
    out_ref[:, :ff] = (silu * up).astype(BF16)
    out_ref[:, ff : 2 * ff] = (dhid * up * slope).astype(BF16)
    out_ref[:, 2 * ff :] = (dhid * silu).astype(BF16)


def second_kernel(n_blk, n_sub, n_recv, *refs):
    recv = [views(refs[:n_recv], n_blk), views(refs[n_recv : 2 * n_recv], n_blk)]
    weight_refs = refs[2 * n_recv : 2 * n_recv + 6]
    act_refs, send_ref, rows_ref = refs[-4:-2], refs[-2], refs[-1]
    rows = n_sub * CAP
    ff = weight_refs[0].shape[0]
    out, inp = 0.0, 0.0
    for half in range(2):
        for mb in range(n_blk):
            start = block_start(mb, rows, n_blk)
            rows_ref[half, pl.ds(start, rows), :] = recv[half][mb][...].astype(F32)
        act_refs[half][...] = rows_ref[half].astype(BF16)
        wg_ref, wu_ref, wd_ref = weight_refs[3 * half : 3 * half + 3]
        out = out + dot(act_refs[half][:, :ff], wd_ref[...])
        inp = inp + dot(act_refs[half][:, ff : 2 * ff], wg_ref[...])
        inp = inp + dot(act_refs[half][:, 2 * ff :], wu_ref[...])
    order = pair_matrix(n_sub, True)
    for mb in range(n_blk):
        lower, upper = mb * rows, (mb + 1) * rows
        block = jnp.concatenate([out[lower:upper], inp[lower:upper]], axis=0).astype(BF16)
        moved = dot(order, block)
        for ms in range(n_sub):
            send_ref[mb * n_sub + ms] = moved[ms * 2 * CAP : (ms + 1) * 2 * CAP].astype(BF16)


def grad_kernel(scale, own_ref, peer_ref, both_ref, peer_both_ref, gg_ref, gu_ref, gd_ref):
    total = own_ref.shape[0]
    ff = own_ref.shape[1] // 3
    for i, (out_ref, lower) in enumerate(((gd_ref, total), (gg_ref, 0), (gu_ref, 0))):
        left = own_ref[:, i * ff : (i + 1) * ff]
        left_peer = peer_ref[:, i * ff : (i + 1) * ff]
        right = both_ref[lower : lower + total, :]
        right_peer = peer_both_ref[lower : lower + total, :]
        out_ref[0] = (dot(left, right, 0, 0) + dot(left_peer, right_peer, 0, 0)) * scale


def mix_kernel(n_blk, n_sub, ids_ref, gate_ref, cotan_ref, recv_ref, mixed_ref, grad_ref, gate_grad_ref):
    tok, depth = cotan_ref.shape
    width = depth // n_blk
    placed, weight, part, second = slot_rows(ids_ref, gate_ref, n_sub)
    first_rows = jnp.where(second, 0.0, placed)
    last_rows = jnp.where(second, placed, 0.0)
    pick_in = last_rows.T.astype(BF16)
    pick_out, weights, dots = [], [], []
    for ms in range(n_sub):
        mine = jnp.where(part == ms, first_rows, 0.0)
        pick_out.append(mine.T.astype(BF16))
        weights.append(jnp.sum((mine * weight).T, axis=1, keepdims=True))
        dots.append(jnp.zeros((tok, 1), F32))
    for mb in range(n_blk):
        columns = pl.ds(mb * width, width)
        block = jnp.concatenate(
            [recv_ref[mb * n_sub + ms].astype(F32) for ms in range(n_sub)], axis=0
        ).astype(BF16)
        grad_ref[:, columns] = dot(pick_in, block).astype(BF16)
        cotan = cotan_ref[:, columns].astype(F32)
        mixed = jnp.zeros((tok, width), F32)
        for ms in range(n_sub):
            rows = dot(pick_out[ms], block)
            mixed = mixed + weights[ms] * rows
            dots[ms] = dots[ms] + jnp.sum(rows * cotan, axis=1, keepdims=True)
        mixed_ref[:, columns] = mixed.astype(BF16)
    same = iota((tok, tok), 0) == iota((tok, tok), 1)
    gate_grad = jnp.zeros(ids_ref.shape, F32)
    for ms in range(n_sub):
        line = jnp.sum(jnp.where(same, dots[ms], 0.0), axis=0, keepdims=True)
        hit = ids_ref[...] == ms
        gate_grad = gate_grad + jnp.where(hit, line, 0.0)
    gate_grad_ref[...] = gate_grad


def call(kernel, out, args, scratch=(), flops=0, in_spaces=None, out_spaces=None, sems=0, limit=None):
    def size(x):
        total = jnp.dtype(x.dtype).itemsize
        for d in x.shape:
            total *= d
        return total

    vmem = pltpu.VMEM
    in_spaces = in_spaces or {}
    out_spaces = out_spaces or {}
    moved = sum(size(x) for x in args) + sum(size(x) for x in out)
    held = sum(size(x) for x in scratch)
    limit = limit or min(60 << 20, max(16 << 20, 3 * (moved + held)))
    return pl.pallas_call(
        kernel,
        out_shape=out,
        in_specs=[pl.BlockSpec(memory_space=in_spaces.get(i, vmem)) for i in range(len(args))],
        out_specs=[pl.BlockSpec(memory_space=out_spaces.get(i, vmem)) for i in range(len(out))],
        scratch_shapes=[pltpu.VMEM(x.shape, x.dtype) for x in scratch]
        + ([pltpu.SemaphoreType.DMA((sems,))] if sems else []),
        compiler_params=pltpu.CompilerParams(vmem_limit_bytes=limit),
        cost_estimate=pl.CostEstimate(flops=flops, bytes_accessed=moved, transcendentals=0),
    )(*args)


def array(shape, dtype=BF16):
    return jax.ShapeDtypeStruct(shape, dtype)


def swap(x, axes, count, mask):
    return lax.ppermute(x, axes, [(i, i ^ mask) for i in range(count)])


def on_device(tokens, expert_ids, gate_weights, w_gate, w_up, w_down, cotangent):
    tok, depth = tokens.shape
    top_k = expert_ids.shape[1]
    n_blk, n_sub, n_rep = (lax.axis_size(a) for a in ("blk", "sub", "rep"))
    assert w_gate.shape[0] == 1 and n_rep == 2
    assert n_blk & (n_blk - 1) == 0 and n_sub & (n_sub - 1) == 0
    ff, width = w_gate.shape[1:]
    n = n_blk * n_sub
    direct = n_blk <= MAX_DIRECT
    masks = ORDER if n_blk == 4 else list(range(1, n_blk))
    scale = (tok * n * n_rep * top_k / NUM_EXPERTS) ** (-0.5)
    rows = n_sub * CAP
    total = n_blk * rows
    hbm = pltpu.HBM
    ids, gates = expert_ids.T, gate_weights.T
    weights = [w[0] for w in (w_gate, w_up, w_down)]
    peer_weights = [swap(w, "rep", 2, 1) for w in weights]

    def pair_exchange(x):
        return lax.all_to_all(x, ("blk", "sub"), split_axis=0, concat_axis=0, tiled=True)

    def blk_exchange(parts):
        if not direct:
            return [lax.all_to_all(parts[0], "blk", split_axis=0, concat_axis=0, tiled=True)]
        moved = {m: swap(parts[m], "blk", n_blk, m) for m in masks}
        return [parts[0]] + [moved[m] for m in range(1, n_blk)]

    def blk_gather(x):
        if not direct:
            return [lax.all_gather(x, "blk", axis=0, tiled=False)]
        moved = {m: swap(x, "blk", n_blk, m) for m in masks}
        return [x] + [moved[m] for m in range(1, n_blk)]

    parts_out = [array((rows, 3 * ff))] * n_blk if direct else [array((n_blk, rows, 3 * ff))]
    flops = 2 * total * width * 3 * ff
    sent = call(
        functools.partial(route_kernel, n_blk, n_sub),
        [array((n, 2 * CAP, width))],
        [ids, gates, tokens, cotangent],
        scratch=[ids, gates, tokens, cotangent],
        in_spaces={0: hbm, 1: hbm, 2: hbm, 3: hbm},
        limit=60 << 20,
        sems=2 + 2 * n_blk,
    )[0]
    got = pair_exchange(sent)
    both, *parts = call(
        functools.partial(first_kernel, n_blk, n_sub),
        [array((2 * total, width))] + parts_out,
        [got] + weights,
        scratch=[array((total, 3 * ff), F32), array((2 * total, width), F32)],
        flops=flops,
    )
    peer_parts = call(
        functools.partial(peer_kernel, n_blk),
        parts_out,
        [both] + peer_weights,
        scratch=[array((total, 3 * ff), F32)],
        flops=flops,
    )
    both_peer = swap(both, "rep", 2, 1)
    acts = []
    for part in (parts, peer_parts):
        summed = call(
            functools.partial(act_kernel, n_blk), [array((rows, 3 * ff))], blk_exchange(part)
        )[0]
        acts.append(blk_gather(summed))
    own, other, sent = call(
        functools.partial(second_kernel, n_blk, n_sub, len(acts[0])),
        [array((total, 3 * ff))] * 2 + [array((n, 2 * CAP, width))],
        acts[0] + acts[1] + weights + peer_weights,
        scratch=[array((2, total, 3 * ff), F32)],
        flops=2 * flops,
    )
    got = pair_exchange(sent)
    peer = swap(other, "rep", 2, 1)
    grads = call(
        functools.partial(grad_kernel, scale),
        [array((1, ff, width), F32)] * 3,
        [own, peer, both, both_peer],
        flops=2 * flops,
    )
    mixed, token_grad, gate_grad = call(
        functools.partial(mix_kernel, n_blk, n_sub),
        [array((tok, depth)), array((tok, depth)), array((top_k, tok), F32)],
        [ids, gates, cotangent, got],
    )
    return (mixed, token_grad, gate_grad.T, *grads)


def solution(mesh):
    by_token = P(("dom", "blk", "sub", "rep"), None)
    by_weight = P("sub", "rep", "blk")
    by_grad = P(("dom", "sub"), "rep", "blk")
    return jax.shard_map(
        on_device,
        mesh=mesh,
        in_specs=(by_token, by_token, by_token, by_weight, by_weight, by_weight, by_token),
        out_specs=(by_token, by_token, by_token, by_grad, by_grad, by_grad),
        check_vma=False,
    )
```

```python
import functools

import jax
import jax.numpy as jnp
from jax import lax
from jax.experimental import pallas as pl
from jax.experimental.pallas import tpu as pltpu
from jax.sharding import PartitionSpec as P


NUM_EXPERTS = 128
CAP = 12
MAX_DIRECT = 8
ORDER = [2, 3, 1]
RELAY = (False, False)


F32 = jnp.float32
BF16 = jnp.bfloat16


def iota(shape, dim):
    return lax.broadcasted_iota(jnp.int32, shape, dim)


def group_of(index, size, groups):
    result = jnp.zeros_like(index)
    for start in range(1, groups):
        result = result + (index >= start * size).astype(jnp.int32)
    return result


def dot(a, b, ca=1, cb=0):
    return lax.dot_general(a, b, (((ca,), (cb,)), ((), ())), preferred_element_type=F32)


def slot_rows(ids_ref, gate_ref, n_sub):
    top_k, tok = ids_ref.shape
    n_rows = n_sub * 2 * CAP
    row = iota((n_rows, tok), 0)
    part = group_of(row, 2 * CAP, n_sub)
    rest = row - part * (2 * CAP)
    second = rest >= CAP
    slot = rest - jnp.where(second, CAP, 0)
    picked = jnp.zeros((n_rows, tok), F32)
    weight = jnp.zeros((n_rows, tok), F32)
    for k in range(top_k):
        hit = ids_ref[k : k + 1, :] == part
        picked = picked + jnp.where(hit, 1.0, 0.0)
        weight = weight + jnp.where(hit, gate_ref[k : k + 1, :], 0.0)
    earlier = (iota((tok, tok), 0) < iota((tok, tok), 1)).astype(F32).astype(BF16)
    before = dot(picked.astype(BF16), earlier)
    placed = (before == slot.astype(F32)) & (picked > 0.5)
    return jnp.where(placed, 1.0, 0.0), weight, part, second


def pair_matrix(n_sub, back):
    n = n_sub * 2 * CAP
    out_row, in_row = iota((n, n), 0), iota((n, n), 1)
    mixed_row, plain_row = (in_row, out_row) if back else (out_row, in_row)
    kind = (mixed_row >= n_sub * CAP).astype(jnp.int32)
    rest = mixed_row - kind * (n_sub * CAP)
    where_to = rest + CAP * group_of(rest, CAP, n_sub) + CAP * kind
    return (where_to == plain_row).astype(F32).astype(BF16)


def route_kernel(n_blk, n_sub, ids_ref, gate_ref, tokens_ref, cotan_ref, send_ref):
    width = tokens_ref.shape[1] // n_blk
    placed, weight, _, second = slot_rows(ids_ref, gate_ref, n_sub)
    gate = jnp.sum(placed * weight, axis=1, keepdims=True)
    low = placed.astype(BF16)
    is_cotan = second[:, :1]
    for mb in range(n_blk):
        columns = pl.ds(mb * width, width)
        rows = dot(low, tokens_ref[:, columns])
        dout = dot(low, cotan_ref[:, columns]) * gate
        block = jnp.where(is_cotan, dout, rows)
        for ms in range(n_sub):
            send_ref[mb * n_sub + ms] = block[ms * 2 * CAP : (ms + 1) * 2 * CAP].astype(BF16)


def views(refs, count):
    return list(refs) if len(refs) > 1 or count == 1 else [refs[0].at[i] for i in range(count)]


def block_start(mb, rows, n_blk):
    if n_blk > MAX_DIRECT:
        return mb * rows
    return pl.multiple_of(lax.bitwise_xor(lax.axis_index("blk").astype(jnp.int32), mb) * rows, 8)


def partial_products(n_blk, both_ref, weight_refs, part_ref, sends):
    total = both_ref.shape[0] // 2
    rows = total // n_blk
    ff = weight_refs[0].shape[0]
    toks, dout = both_ref[:total, :], both_ref[total:, :]
    for i, left in enumerate((toks, toks, dout)):
        part_ref[:, i * ff : (i + 1) * ff] = dot(left, weight_refs[i][...], 1, 1)
    for mb in range(n_blk):
        start = block_start(mb, rows, n_blk)
        sends[mb][...] = part_ref[pl.ds(start, rows), :].astype(BF16)


def first_kernel(n_blk, n_sub, recv_ref, *refs):
    weight_refs, both_ref = refs[:3], refs[3]
    sends, (part_ref, rows_ref) = views(refs[4:-2], n_blk), refs[-2:]
    rows = n_sub * CAP
    total = n_blk * rows
    order = pair_matrix(n_sub, False)
    for mb in range(n_blk):
        block = jnp.concatenate([recv_ref[mb * n_sub + ms].astype(F32) for ms in range(n_sub)], axis=0)
        moved = dot(order, block.astype(BF16))
        rows_ref[mb * rows : (mb + 1) * rows, :] = moved[:rows]
        rows_ref[total + mb * rows : total + (mb + 1) * rows, :] = moved[rows:]
    both_ref[...] = rows_ref[...].astype(BF16)
    partial_products(n_blk, both_ref, weight_refs, part_ref, sends)


def peer_kernel(n_blk, both_ref, *refs):
    partial_products(n_blk, both_ref, refs[:3], refs[-1], views(refs[3:-1], n_blk))


def act_kernel(n_blk, *refs):
    recv, out_ref = views(refs[:-1], n_blk), refs[-1]
    ff = out_ref.shape[1] // 3
    total = recv[0][...].astype(F32)
    for i in range(1, n_blk):
        total = total + recv[i][...].astype(F32)
    gate, up, dhid = total[:, :ff], total[:, ff : 2 * ff], total[:, 2 * ff :]
    sig = jax.nn.sigmoid(gate)
    silu = gate * sig
    slope = sig * (1.0 + gate * (1.0 - sig))
    out_ref[:, :ff] = (silu * up).astype(BF16)
    out_ref[:, ff : 2 * ff] = (dhid * up * slope).astype(BF16)
    out_ref[:, 2 * ff :] = (dhid * silu).astype(BF16)


def half_products(n_blk, recv, weight_refs, act_ref, rows_ref):
    rows = recv[0].shape[0]
    ff = weight_refs[0].shape[0]
    for mb in range(n_blk):
        rows_ref[pl.ds(block_start(mb, rows, n_blk), rows), :] = recv[mb][...].astype(F32)
    act_ref[...] = rows_ref[...].astype(BF16)
    wg_ref, wu_ref, wd_ref = weight_refs
    out = dot(act_ref[:, :ff], wd_ref[...])
    inp = dot(act_ref[:, ff : 2 * ff], wg_ref[...]) + dot(act_ref[:, 2 * ff :], wu_ref[...])
    return out, inp


def second_kernel(n_blk, n_recv, *refs):
    act_ref, sum_ref, rows_ref = refs[-3:]
    total = act_ref.shape[0]
    out, inp = half_products(n_blk, views(refs[:n_recv], n_blk), refs[n_recv : n_recv + 3], act_ref, rows_ref)
    sum_ref[:total, :] = out
    sum_ref[total:, :] = inp


def third_kernel(n_blk, n_sub, n_recv, *refs):
    sum_ref, act_ref, send_ref, rows_ref = refs[n_recv + 3 :]
    rows = n_sub * CAP
    total = act_ref.shape[0]
    out, inp = half_products(n_blk, views(refs[:n_recv], n_blk), refs[n_recv : n_recv + 3], act_ref, rows_ref)
    out = out + sum_ref[:total, :]
    inp = inp + sum_ref[total:, :]
    order = pair_matrix(n_sub, True)
    for mb in range(n_blk):
        lower, upper = mb * rows, (mb + 1) * rows
        block = jnp.concatenate([out[lower:upper], inp[lower:upper]], axis=0).astype(BF16)
        moved = dot(order, block)
        for ms in range(n_sub):
            send_ref[mb * n_sub + ms] = moved[ms * 2 * CAP : (ms + 1) * 2 * CAP].astype(BF16)


def grad_kernel(scale, n_sub, ids_ref, gate_ref, own_ref, peer_ref, both_ref, peer_both_ref, gg_ref, gu_ref, gd_ref, pick_in_ref, pick_out_ref, column_ref):
    placed, weight, part, second = slot_rows(ids_ref, gate_ref, n_sub)
    first_rows = jnp.where(second, 0.0, placed)
    pick_in_ref[...] = jnp.where(second, placed, 0.0).T.astype(BF16)
    for ms in range(n_sub):
        mine = jnp.where(part == ms, first_rows, 0.0)
        pick_out_ref[ms] = mine.T.astype(BF16)
        column_ref[ms] = jnp.broadcast_to(
            jnp.sum((mine * weight).T, axis=1, keepdims=True), column_ref.shape[1:]
        )
    total = own_ref.shape[0]
    ff = own_ref.shape[1] // 3
    for i, (out_ref, lower) in enumerate(((gd_ref, total), (gg_ref, 0), (gu_ref, 0))):
        left = own_ref[:, i * ff : (i + 1) * ff]
        left_peer = peer_ref[:, i * ff : (i + 1) * ff]
        right = both_ref[lower : lower + total, :]
        right_peer = peer_both_ref[lower : lower + total, :]
        out_ref[0] = (dot(left, right, 0, 0) + dot(left_peer, right_peer, 0, 0)) * scale


def mix_kernel(n_blk, n_sub, ids_ref, cotan_ref, pick_in_ref, pick_out_ref, column_ref, recv_ref, mixed_ref, grad_ref, gate_grad_ref):
    tok, depth = cotan_ref.shape
    width = depth // n_blk
    lanes = column_ref.shape[2]
    dots = [jnp.zeros((tok, lanes), F32) for _ in range(n_sub)]
    for mb in range(n_blk):
        block = jnp.concatenate(
            [recv_ref[mb * n_sub + ms].astype(F32) for ms in range(n_sub)], axis=0
        ).astype(BF16)
        columns = pl.ds(mb * width, width)
        grad_ref[:, columns] = dot(pick_in_ref[...], block).astype(BF16)
        picked = [dot(pick_out_ref[ms], block) for ms in range(n_sub)]
        for lower in range(0, width, lanes):
            columns = pl.ds(mb * width + lower, lanes)
            cotan = cotan_ref[:, columns].astype(F32)
            mixed = jnp.zeros((tok, lanes), F32)
            for ms in range(n_sub):
                rows = picked[ms][:, lower : lower + lanes]
                mixed = mixed + column_ref[ms] * rows
                dots[ms] = dots[ms] + rows * cotan
            mixed_ref[:, columns] = mixed.astype(BF16)
    same = iota((tok, tok), 0) == iota((tok, tok), 1)
    gate_grad = jnp.zeros(ids_ref.shape, F32)
    for ms in range(n_sub):
        total = jnp.sum(dots[ms], axis=1, keepdims=True)
        line = jnp.sum(jnp.where(same, total, 0.0), axis=0, keepdims=True)
        gate_grad = gate_grad + jnp.where(ids_ref[...] == ms, line, 0.0)
    gate_grad_ref[...] = gate_grad


def call(kernel, out, args, scratch=(), flops=0, in_spaces=None, out_spaces=None, sems=0, limit=None):
    def size(x):
        total = jnp.dtype(x.dtype).itemsize
        for d in x.shape:
            total *= d
        return total

    vmem = pltpu.VMEM
    in_spaces = in_spaces or {}
    out_spaces = out_spaces or {}
    moved = sum(size(x) for x in args) + sum(size(x) for x in out)
    held = sum(size(x) for x in scratch)
    limit = limit or min(60 << 20, max(16 << 20, 3 * (moved + held)))
    return pl.pallas_call(
        kernel,
        out_shape=out,
        in_specs=[pl.BlockSpec(memory_space=in_spaces.get(i, vmem)) for i in range(len(args))],
        out_specs=[pl.BlockSpec(memory_space=out_spaces.get(i, vmem)) for i in range(len(out))],
        scratch_shapes=[pltpu.VMEM(x.shape, x.dtype) for x in scratch]
        + ([pltpu.SemaphoreType.DMA((sems,))] if sems else []),
        compiler_params=pltpu.CompilerParams(vmem_limit_bytes=limit),
        cost_estimate=pl.CostEstimate(flops=flops, bytes_accessed=moved, transcendentals=0),
    )(*args)


def array(shape, dtype=BF16):
    return jax.ShapeDtypeStruct(shape, dtype)


def swap(x, axes, count, mask):
    return lax.ppermute(x, axes, [(i, i ^ mask) for i in range(count)])


def layer(tokens, expert_ids, gate_weights, w_gate, w_up, w_down, cotangent):
    tok, depth = tokens.shape
    top_k = expert_ids.shape[1]
    n_blk, n_sub, n_rep = (lax.axis_size(a) for a in ("blk", "sub", "rep"))
    assert w_gate.shape[0] == 1 and n_rep == 2
    assert n_blk & (n_blk - 1) == 0 and n_sub & (n_sub - 1) == 0
    ff, width = w_gate.shape[1:]
    n = n_blk * n_sub
    direct = n_blk <= MAX_DIRECT
    masks = ORDER if n_blk == 4 else list(range(1, n_blk))
    scale = (tok * n * n_rep * top_k / NUM_EXPERTS) ** (-0.5)
    rows = n_sub * CAP
    total = n_blk * rows
    ids, gates = expert_ids.T, gate_weights.T
    weights = [w[0] for w in (w_gate, w_up, w_down)]
    peer_weights = [swap(w, "rep", 2, 1) for w in weights]

    def pair_exchange(x):
        return lax.all_to_all(x, ("blk", "sub"), split_axis=0, concat_axis=0, tiled=True)

    def blk_exchange(parts):
        if not direct:
            return [lax.all_to_all(parts[0], "blk", split_axis=0, concat_axis=0, tiled=True)]
        moved = {m: swap(parts[m], "blk", n_blk, m) for m in masks}
        return [parts[0]] + [moved[m] for m in range(1, n_blk)]

    def blk_gather(x, relay):
        if not direct:
            return [lax.all_gather(x, "blk", axis=0, tiled=False)]
        if relay and n_blk == 4:
            far = swap(x, "blk", n_blk, 2)
            near = swap(x, "blk", n_blk, 1)
            last = swap(far, "blk", n_blk, 1)
            return [x, near, far, last]
        moved = {m: swap(x, "blk", n_blk, m) for m in masks}
        return [x] + [moved[m] for m in range(1, n_blk)]

    parts_out = [array((rows, 3 * ff))] * n_blk if direct else [array((n_blk, rows, 3 * ff))]
    flops = 2 * total * width * 3 * ff
    sent = call(
        functools.partial(route_kernel, n_blk, n_sub),
        [array((n, 2 * CAP, width))],
        [ids, gates, tokens, cotangent],
        limit=60 << 20,
    )[0]
    got = pair_exchange(sent)
    both, *parts = call(
        functools.partial(first_kernel, n_blk, n_sub),
        [array((2 * total, width))] + parts_out,
        [got] + weights,
        scratch=[array((total, 3 * ff), F32), array((2 * total, width), F32)],
        flops=flops,
    )
    peer_parts = call(
        functools.partial(peer_kernel, n_blk),
        parts_out,
        [both] + peer_weights,
        scratch=[array((total, 3 * ff), F32)],
        flops=flops,
    )
    both_peer = swap(both, "rep", 2, 1)
    acts = []
    for part in (parts, peer_parts):
        half = len(acts)
        moved = blk_exchange(part)
        summed = call(functools.partial(act_kernel, n_blk), [array((rows, 3 * ff))], moved)[0]
        acts.append(blk_gather(summed, RELAY[half]))
    own, sums = call(
        functools.partial(second_kernel, n_blk, len(acts[0])),
        [array((total, 3 * ff)), array((2 * total, width), F32)],
        acts[0] + weights,
        scratch=[array((total, 3 * ff), F32)],
        flops=flops,
    )
    other, sent = call(
        functools.partial(third_kernel, n_blk, n_sub, len(acts[1])),
        [array((total, 3 * ff)), array((n, 2 * CAP, width))],
        acts[1] + peer_weights + [sums],
        scratch=[array((total, 3 * ff), F32)],
        flops=flops,
    )
    got = pair_exchange(sent)
    peer = swap(other, "rep", 2, 1)
    *grads, pick_in, pick_out, column = call(
        functools.partial(grad_kernel, scale, n_sub),
        [array((1, ff, width), F32)] * 3
        + [array((tok, 2 * rows)), array((n_sub, tok, 2 * rows)), array((n_sub, tok, 128), F32)],
        [ids, gates, own, peer, both, both_peer],
        flops=2 * flops,
    )
    mixed, token_grad, gate_grad = call(
        functools.partial(mix_kernel, n_blk, n_sub),
        [array((tok, depth)), array((tok, depth)), array((top_k, tok), F32)],
        [ids, cotangent, pick_in, pick_out, column, got],
    )
    return (mixed, token_grad, gate_grad.T, *grads)


def solution(mesh):
    by_token = P(("dom", "blk", "sub", "rep"), None)
    by_weight = P("sub", "rep", "blk")
    by_grad = P(("dom", "sub"), "rep", "blk")
    return jax.shard_map(
        layer,
        mesh=mesh,
        in_specs=(by_token, by_token, by_token, by_weight, by_weight, by_weight, by_token),
        out_specs=(by_token, by_token, by_token, by_grad, by_grad, by_grad),
        check_vma=False,
    )
```
